256 devices in a mesh: seq: 64 (over x_hi, y, z), tp: 4 (over x_lo, core).
Axes of the slice: x: 4 (x_hi: 2, x_lo: 2; x = x_hi * 2 + x_lo), y: 4, z: 8, core: 2. Of those that a mesh axis runs over, the one named last changes fastest.
Arguments:
- features: bfloat16 [16384, 3, 4096], P('seq', None, 'tp'), may hold values from -6 to 6
- short_taps: float32 [3, 7, 4096], P(None, None, 'tp'), may hold values from -2 to 2
- residue: float32 [16, 4096], P(None, 'tp'), may hold values from -1.5 to 1.5
- decay_rate: float32 [16, 4096], P(None, 'tp'), may hold values from 6.1035157e-06 to 0.05
- w_out: bfloat16 [4096, 4096], P('tp', 'seq'), may hold values from -0.09375 to 0.09375
- cotangent: bfloat16 [16384, 4096], P('seq', 'tp'), may hold values from -16 to 16
Outputs:
- mixed: bfloat16 [16384, 4096], P('seq', 'tp')
- grad_features: bfloat16 [16384, 3, 4096], P('seq', None, 'tp')
- grad_weight: float32 [4096, 4096], P('tp', 'seq')
- grad_taps: float32 [3, 7, 4096], P(None, None, 'tp')
- grad_residue: float32 [16, 4096], P(None, 'tp')
- grad_log_rate: float32 [16, 4096], P(None, 'tp')
The draws below stay inside these ranges and needn't reach their ends.
All inputs are finite; a program needn't handle non-finite values.
Results may differ from the reference program's by a relative error of at most 0.013.
Values may be sent and summed in bfloat16 or wider, within the bound.
No kernel may reach another device: no remote copies, remote signals or barrier semaphores. Data moves between devices by JAX's collectives and lax.ppermute only.
A program may use at most 128 MiB of HBM per device.

```python
import math
import jax
import jax.numpy as jnp
from jax import lax

D = 4096
MODES = 16
TAPS = 7
TOKENS = 16384
N_TP = 4


def with_spikes(array, rng, source, target, parts, factor):
    owner, partner = [(jnp.arange(array.shape[position]) // (array.shape[position] // parts)).reshape([-1 if axis == position else 1 for axis in range(array.ndim)]) for position in (source, target)]
    chosen = jax.random.permutation(rng, parts)[partner]
    strong = (owner == chosen) | (owner == (partner + parts // 2) % parts)
    return jnp.where(strong, factor * array, array)


def block_levels(key, extent, shards, low, top_value):
    factor_of, own = 1.0, jax.random.fold_in(key, 6)
    for dim, blocks in shards:
        draws = jnp.exp(jax.random.uniform(jax.random.fold_in(own, dim), (blocks,), jnp.float32, low / len(shards), top_value / len(shards)))
        factor_of = factor_of * jnp.repeat(draws, extent[dim] // blocks).reshape([-1 if axis == dim else 1 for axis in range(len(extent))])
    return factor_of


def normal_values(rng, shape, scale, limit, split=(), kind=jnp.bfloat16):
    entries = scale * jax.random.normal(rng, shape, jnp.float32)
    if split:
        entries = entries * block_levels(rng, shape, split, -0.22, 0.18)
    return jnp.clip(entries, -limit, limit).astype(kind)


def noise_with(stream_key, dims, deviation, most, shards, heavy, kind=jnp.bfloat16):
    drawn = deviation * jax.random.normal(stream_key, dims, jnp.float32)
    if shards:
        drawn = drawn * block_levels(stream_key, dims, shards, -0.22, 0.18)
    return jnp.clip(with_spikes(drawn, jax.random.fold_in(stream_key, 3), *heavy), -most, most).astype(kind)


def setup_inputs(seed: int = 0) -> dict:
    seeds = jax.random.split(jax.random.key(seed), 7)
    features = normal_values(seeds[0], (TOKENS, 3, D), 1.0, 6.0, ((0, 64), (2, 4)))
    short_taps = normal_values(seeds[1], (3, TAPS, D), TAPS ** -0.5, 2.0, ((2, 4),), jnp.float32)
    residue = normal_values(seeds[2], (MODES, D), MODES ** -0.5, 1.5, ((1, 4),), jnp.float32)
    decay_rate = jnp.clip(jnp.exp(math.log(0.05) - 9.010913 * jax.random.uniform(seeds[3], (MODES, D), jnp.float32) ** block_levels(seeds[3], (MODES, D), ((1, 4),), -0.2, 0.2)), 6.10351571594947e-06, 0.05)
    w_out = normal_values(seeds[4], (D, D), D ** -0.5, 0.09375, ((0, 4), (1, 64)))
    cotangent = noise_with(seeds[5], (TOKENS, D), 1.0, 16.0, ((0, 64), (1, 4)), (0, 1, 64, 4.0))
    return {"features": features, "short_taps": short_taps, "residue": residue, "decay_rate": decay_rate, "w_out": w_out, "cotangent": cotangent}


def short_conv(stream, taps):
    tok_total = stream.shape[0]
    tap_reach = taps.shape[0] - 1
    padded = jnp.pad(stream, ((tap_reach, 0), (0, 0)))
    result = taps[0] * stream.astype(jnp.float32)
    for tap_index in range(1, tap_reach + 1):
        result = result + taps[tap_index] * padded[tap_reach - tap_index:tap_reach - tap_index + tok_total].astype(jnp.float32)
    return result

def short_conv_back(grads, stream, taps):
    tok_total = grads.shape[0]
    tap_reach = taps.shape[0] - 1
    grads_wide = grads.astype(jnp.float32)
    stream_wide = stream.astype(jnp.float32)
    ahead = jnp.pad(grads_wide, ((0, tap_reach), (0, 0)))
    behind = jnp.pad(stream_wide, ((tap_reach, 0), (0, 0)))
    result = taps[0] * grads_wide
    tap_rows = [jnp.einsum('tc,tc->c', grads_wide, stream_wide)]
    for tap_index in range(1, tap_reach + 1):
        result = result + taps[tap_index] * ahead[tap_index:tap_index + tok_total]
        tap_rows.append(jnp.einsum('tc,tc->c', grads_wide, behind[tap_reach - tap_index:tap_reach - tap_index + tok_total]))
    return (result.astype(jnp.bfloat16), jnp.stack(tap_rows, axis=0))

def block_conv(signal, residue, rate):
    length = signal.shape[1]
    lag_values = jnp.arange(length, dtype=jnp.float32)
    coeffs = residue * jnp.sqrt(-jnp.expm1(-2.0 * rate))
    kernel = lax.optimization_barrier(jnp.sum(coeffs[:, :, None] * jnp.exp(-rate[:, :, None] * lag_values[None, None, :]), axis=0))
    padded_len = 2 * length
    spectrum = jnp.fft.rfft(signal, n=padded_len) * jnp.fft.rfft(kernel, n=padded_len)
    return jnp.fft.irfft(spectrum, n=padded_len)[:, :length]

def block_step(inputs):
    signal, upstream, residue, rate = inputs
    output, pullback = jax.vjp(block_conv, signal, residue, rate)
    grad_signal, grad_res, grad_rate = pullback(upstream)
    return (output, grad_signal, grad_res, grad_rate)

def split_channels(matrix, block_width):
    leading = matrix.shape[0]
    return jnp.transpose(matrix.reshape(leading, -1, block_width), (1, 0, 2))

def join_channels(blocks):
    return jnp.transpose(blocks, (1, 0, 2)).reshape(blocks.shape[1], -1)

def reference(features, short_taps, residue, decay_rate, w_out, cotangent):
    tok_total = features.shape[0]
    channel_count = features.shape[2]
    query_part = short_conv(features[:, 0, :], short_taps[0])
    keyed = short_conv(features[:, 1, :], short_taps[1])
    valued = short_conv(features[:, 2, :], short_taps[2])
    product = (keyed * valued).astype(jnp.bfloat16)
    grad_gated = jnp.dot(cotangent, w_out.T, preferred_element_type=jnp.float32).astype(jnp.bfloat16)
    grad_conv = (grad_gated * query_part).astype(jnp.bfloat16)
    block_width = min(64, channel_count)
    sig_blocks = product.T.astype(jnp.float32).reshape(-1, block_width, tok_total)
    up_blocks = grad_conv.T.astype(jnp.float32).reshape(-1, block_width, tok_total)
    conv_blocks, grad_blocks, res_blocks, rate_blocks = lax.map(block_step, (sig_blocks, up_blocks, split_channels(residue, block_width), split_channels(decay_rate, block_width)))
    convolved = conv_blocks.reshape(channel_count, tok_total).T.astype(jnp.bfloat16)
    grad_product = grad_blocks.reshape(channel_count, tok_total).T.astype(jnp.bfloat16)
    grad_residue = join_channels(res_blocks)
    grad_log_rate = join_channels(rate_blocks) * decay_rate
    gated = (query_part * convolved).astype(jnp.bfloat16)
    group_width = channel_count // N_TP
    mixed_total = jnp.zeros((tok_total, channel_count), jnp.float32)
    for group_index in range(N_TP):
        lower_edge = group_index * group_width
        partial_out = jnp.dot(gated[:, lower_edge:lower_edge + group_width], w_out[lower_edge:lower_edge + group_width], preferred_element_type=jnp.float32)
        rounded = lax.optimization_barrier(partial_out.astype(jnp.bfloat16))
        mixed_total = mixed_total + rounded.astype(jnp.float32)
    mixed = mixed_total.astype(jnp.bfloat16)
    grad_weight = jnp.dot(gated.T, cotangent, preferred_element_type=jnp.float32)
    grad_query = (grad_gated * convolved).astype(jnp.bfloat16)
    grad_key = (grad_product * valued).astype(jnp.bfloat16)
    grad_value = (grad_product * keyed).astype(jnp.bfloat16)
    feat_query, taps_query = short_conv_back(grad_query, features[:, 0, :], short_taps[0])
    feat_key, taps_key = short_conv_back(grad_key, features[:, 1, :], short_taps[1])
    feat_value, taps_value = short_conv_back(grad_value, features[:, 2, :], short_taps[2])
    grad_features = jnp.stack([feat_query, feat_key, feat_value], axis=1)
    grad_taps = jnp.stack([taps_query, taps_key, taps_value], axis=0)
    return (mixed, grad_features, grad_weight, grad_taps, grad_residue, grad_log_rate)
```

```python
import jax
import jax.numpy as jnp
from jax import lax
from jax.experimental import pallas as pl
from jax.experimental.pallas import tpu as pltpu
from jax.sharding import Mesh, PartitionSpec as P

F32 = jnp.float32
BF16 = jnp.bfloat16
SEQ = ("xh", "y", "z")
NX, NY, NZ = 2, 4, 8
SLABS = NX * NY * NZ
SUB = 8
LANES = 128
GROUPS = 1
HIGH = dict(exponent_bits=8, mantissa_bits=7)


def spread(row):
    return jnp.broadcast_to(row, (SUB, LANES))


def sub_index():
    return lax.broadcasted_iota(jnp.int32, (SUB, LANES), 0)


def earlier_sum(ends, decay):
    index = sub_index()

    def moved(value, by):
        return jnp.where(index >= by, pltpu.roll(value, by, 0), 0.0)

    total = moved(ends, 1)
    factor = decay
    for by in (1, 2, 4):
        total = total + factor * moved(total, by)
        factor = factor * factor
    return total


def later_sum(ends, decay):
    index = sub_index()

    def moved(value, by):
        return jnp.where(index < SUB - by, pltpu.roll(value, SUB - by, 0), 0.0)

    total = moved(ends, 1)
    factor = decay
    for by in (1, 2, 4):
        total = total + factor * moved(total, by)
        factor = factor * factor
    return total


def lane_groups(run):
    def kernel(*refs):
        width = refs[0].shape[1]
        for group in range(width // LANES):
            column = pl.program_id(0) * (width // LANES) + group
            run(pl.ds(group * LANES, LANES), column, *refs)

    return kernel


def decays(rate_ref, lanes, modes):
    return [spread(jnp.exp(-rate_ref[m : m + 1, lanes])) for m in modes]


def local_states_kernel(backward, lanes, column, signal_ref, rate_ref, end_ref, enter_ref):
    modes = rate_ref.shape[0]
    steps = signal_ref.shape[0] // SUB
    decay = decays(rate_ref, lanes, range(modes))

    def step(i, states):
        at = steps - 1 - i if backward else i
        value = signal_ref[pl.ds(at, SUB, stride=steps), lanes]
        return tuple(decay[m] * states[m] + value for m in range(modes))

    zero = jnp.zeros((SUB, LANES), F32)
    states = lax.fori_loop(0, steps, step, (zero,) * modes, unroll=8)
    index = sub_index().astype(F32)
    distance = index if backward else (SUB - 1.0) - index
    for m in range(modes):
        rate = spread(rate_ref[m : m + 1, lanes]) * steps
        weighted = jnp.exp(-rate * distance) * states[m]
        end_ref[m, pl.ds(column, 1), :] = jnp.sum(weighted, axis=0, keepdims=True)
        join = later_sum if backward else earlier_sum
        enter_ref[m, :, lanes] = join(states[m], jnp.exp(-rate))


def start_states(lanes, column, rate_ref, enter_ref, outer_ref, steps, backward, m):
    index = sub_index().astype(F32)
    distance = (SUB - 1.0) - index if backward else index
    rate = spread(rate_ref[m : m + 1, lanes]) * steps
    outer = spread(outer_ref[m, pl.ds(column, 1), :])
    return enter_ref[m, :, lanes] + jnp.exp(-rate * distance) * outer


def output_steps(backward, lanes, signal_ref, decay, coeff, start, out_ref):
    steps = signal_ref.shape[0] // SUB
    modes = len(decay)

    def step(i, states):
        at = steps - 1 - i if backward else i
        value = signal_ref[pl.ds(at, SUB, stride=steps), lanes]
        states = tuple(decay[m] * states[m] + value for m in range(modes))
        terms = [coeff[m] * states[m] for m in range(modes)]
        while len(terms) > 1:
            terms = [terms[j] + terms[j + 1] for j in range(0, len(terms), 2)]
        out_ref[pl.ds(at, SUB, stride=steps), lanes] = terms[0]
        return states

    lax.fori_loop(0, steps, step, start, unroll=4)


def forward_kernel(lanes, column, signal_ref, rate_ref, coeff_ref, enter_ref, outer_ref, out_ref):
    modes = rate_ref.shape[0]
    steps = signal_ref.shape[0] // SUB
    decay = decays(rate_ref, lanes, range(modes))
    coeff = [spread(coeff_ref[m : m + 1, lanes]) for m in range(modes)]
    start = tuple(
        start_states(lanes, column, rate_ref, enter_ref, outer_ref, steps, False, m) for m in range(modes)
    )
    output_steps(False, lanes, signal_ref, decay, coeff, start, out_ref)


def backward_kernel(
    lanes,
    column,
    signal_ref,
    rate_ref,
    coeff_ref,
    enter_ref,
    outer_ref,
    slope_ref,
    partial_ref,
    out_ref,
    beta_ref,
):
    modes = rate_ref.shape[0]
    steps = signal_ref.shape[0] // SUB
    decay = decays(rate_ref, lanes, range(modes))
    coeff = [spread(coeff_ref[m : m + 1, lanes]) for m in range(modes)]
    start = tuple(
        start_states(lanes, column, rate_ref, enter_ref, outer_ref, steps, True, m) for m in range(modes)
    )
    for m in range(modes):
        crossing = jnp.sum(decay[m] * slope_ref[m, :, lanes] * start[m], axis=0, keepdims=True)
        beta_ref[m, pl.ds(column, 1), :] = partial_ref[m, pl.ds(column, 1), :] + crossing
    output_steps(True, lanes, signal_ref, decay, coeff, start, out_ref)


def sums_kernel(
    lanes, column, signal_ref, grad_ref, rate_ref, enter_ref, outer_ref, alpha_ref, partial_ref, slope_ref
):
    modes = rate_ref.shape[0]
    steps = signal_ref.shape[0] // SUB
    zero = jnp.zeros((SUB, LANES), F32)
    group = 8
    for first in range(0, modes, group):
        decay = decays(rate_ref, lanes, range(first, first + group))
        start = tuple(
            start_states(lanes, column, rate_ref, enter_ref, outer_ref, steps, False, first + m)
            for m in range(group)
        )

        def step(i, carry):
            states, slopes, alphas, betas = carry
            value = signal_ref[pl.ds(i, SUB, stride=steps), lanes]
            grad = grad_ref[pl.ds(i, SUB, stride=steps), lanes]
            slopes = tuple(decay[m] * slopes[m] + states[m] for m in range(group))
            states = tuple(decay[m] * states[m] + value for m in range(group))
            alphas = tuple(alphas[m] + grad * states[m] for m in range(group))
            betas = tuple(betas[m] + grad * slopes[m] for m in range(group))
            return states, slopes, alphas, betas

        zeros = (zero,) * group
        _, slopes, alphas, betas = lax.fori_loop(0, steps, step, (start, zeros, zeros, zeros), unroll=4)
        for m in range(group):
            row = first + m
            alpha_ref[row, pl.ds(column, 1), :] = jnp.sum(alphas[m], axis=0, keepdims=True)
            partial_ref[row, pl.ds(column, 1), :] = jnp.sum(betas[m], axis=0, keepdims=True)
            slope_ref[row, :, lanes] = slopes[m]


def modal_call(body, name, work, inputs, outputs):
    tokens, channels = inputs[0][1].shape
    modes = inputs[-1][1].shape[0]
    block = LANES * GROUPS
    blocks = {
        "tokens": pl.BlockSpec((tokens, block), lambda c: (0, c)),
        "modes": pl.BlockSpec((modes, block), lambda c: (0, c)),
        "subs": pl.BlockSpec((modes, SUB, block), lambda c: (0, 0, c)),
        "rows": pl.BlockSpec((modes, channels // LANES, LANES), lambda c: (0, 0, 0)),
    }
    shapes = {
        "tokens": (tokens, channels),
        "subs": (modes, SUB, channels),
        "rows": (modes, channels // LANES, LANES),
    }
    return pl.pallas_call(
        lane_groups(body),
        name=name,
        grid=(channels // block,),
        in_specs=[blocks[kind] for kind, _ in inputs],
        out_specs=[blocks[kind] for kind in outputs],
        out_shape=[jax.ShapeDtypeStruct(shapes[kind], F32) for kind in outputs],
        cost_estimate=pl.CostEstimate(
            flops=work * modes * tokens * channels, transcendentals=0, bytes_accessed=8 * tokens * channels
        ),
    )(*[array for _, array in inputs])


def local_states(signal, rates, backward):
    return modal_call(
        lambda *refs: local_states_kernel(backward, *refs),
        "adjoint_ends" if backward else "state_ends",
        2,
        [("tokens", signal), ("modes", rates)],
        ["rows", "subs"],
    )


def forward_output(signal, rates, coeffs, enter, outer):
    inputs = [("tokens", signal), ("modes", rates), ("modes", coeffs), ("subs", enter), ("rows", outer)]
    return modal_call(forward_kernel, "modal_forward", 4, inputs, ["tokens"])[0]


def backward_output(signal, rates, coeffs, enter, outer, slopes, partial):
    inputs = [("tokens", signal), ("modes", rates), ("modes", coeffs), ("subs", enter), ("rows", outer)]
    inputs += [("subs", slopes), ("rows", partial)]
    return modal_call(backward_kernel, "modal_backward", 4, inputs, ["tokens", "rows"])


def mode_sums(signal, grads, rates, enter, outer):
    inputs = [("tokens", signal), ("tokens", grads), ("modes", rates), ("subs", enter), ("rows", outer)]
    return modal_call(sums_kernel, "mode_sums", 8, inputs, ["rows", "rows", "subs"])


def slab_scan_kernel(backward, ends_ref, decay_ref, out_ref):
    decay = decay_ref[...]
    state = jnp.zeros(decay.shape, F32)
    order = range(SLABS - 1, -1, -1) if backward else range(SLABS)
    for slab in order:
        out_ref[slab] = state
        state = decay * state + ends_ref[slab]


def entering(ends, slab_decay, backward, beside):
    shape = (SLABS, ends.size // SLABS // LANES, LANES)
    mine = lax.axis_index(SEQ)
    decay = lax.dynamic_index_in_dim(slab_decay.reshape(shape), mine, 0, keepdims=False)
    gathered = lax.all_to_all(ends.reshape(shape), SEQ, 0, 0, tiled=True)
    gathered, beside = lax.optimization_barrier((gathered, beside))
    scanned = pl.pallas_call(
        lambda *refs: slab_scan_kernel(backward, *refs),
        name="slab_scan_back" if backward else "slab_scan",
        out_shape=jax.ShapeDtypeStruct(shape, F32),
        cost_estimate=pl.CostEstimate(
            flops=2 * ends.size, transcendentals=0, bytes_accessed=8 * ends.size
        ),
    )(gathered, decay)
    outer = lax.all_to_all(scanned, SEQ, 0, 0, tiled=True).reshape(ends.shape)
    return outer, beside


def ring(array, axis, size, by):
    return lax.ppermute(array, axis, [(i, (i + by) % size) for i in range(size)])


def gather_weight(w_rows):
    other = ring(w_rows, "xh", NX, 1)
    first = lax.axis_index("xh") == 0
    pair = jnp.concatenate([jnp.where(first, w_rows, other), jnp.where(first, other, w_rows)], axis=0)
    return lax.all_gather(pair, ("y", "z"), axis=0, tiled=True)


def to_gather_order(rows):
    tokens, width = rows.shape
    cols = width // SLABS
    return rows.reshape(tokens, NX, NY * NZ, cols).transpose(0, 2, 1, 3).reshape(tokens, width)


def from_gather_order(rows):
    tokens, width = rows.shape
    cols = width // SLABS
    return rows.reshape(tokens, NY * NZ, NX, cols).transpose(0, 2, 1, 3).reshape(tokens, width)


def gather_columns(block):
    size = lax.axis_size("tp")
    width = block.shape[1]
    own = lax.axis_index("tp")
    whole = jnp.zeros((block.shape[0], size * width), block.dtype)
    for offset in range(size):
        part = ring(block, "tp", size, -offset) if offset else block
        whole = lax.dynamic_update_slice_in_dim(whole, part, (own + offset) % size * width, 1)
    return whole


def shifted(array, by):
    pairs = [(i, i + by) for i in range(SLABS) if 0 <= i + by < SLABS]
    return lax.ppermute(array, SEQ, pairs)


def to_ring_order(rows):
    tokens, width = rows.shape
    cols = width // SLABS
    return rows.reshape(tokens, NX * NY, NZ, cols).transpose(0, 2, 1, 3).reshape(tokens, width)


def weight_grad(term):
    cols, channels = term.shape[0] // SLABS, term.shape[1]
    summed = lax.psum_scatter(term, "z", scatter_dimension=0, tiled=True)
    by_y = summed.reshape(NX, NY, cols, channels)
    own = lax.axis_index("y")

    def block(target):
        return lax.dynamic_index_in_dim(by_y, target % NY, 1, keepdims=False)

    total = block(own).astype(F32)
    for offset in range(1, NY):
        total = total + ring(block(own - offset), "y", NY, -offset).astype(F32)
    mine = lax.axis_index("xh")
    away = ring(lax.dynamic_index_in_dim(total, 1 - mine, 0, keepdims=False), "xh", NX, 1)
    return (lax.dynamic_index_in_dim(total, mine, 0, keepdims=False) + away).T


def total_over_slabs(rows):
    count, channels = rows.shape
    shape = (SLABS, count * channels // SLABS // LANES, LANES)
    pieces = lax.all_to_all(rows.reshape(shape), SEQ, 0, 0, tiled=True)
    summed = jnp.sum(pieces, axis=0)
    copies = jnp.broadcast_to(summed[None], shape)
    return lax.all_to_all(copies, SEQ, 0, 0, tiled=True).reshape(count, channels)


def local(features, short_taps, residue, decay_rate, w_out, cotangent):
    tok_count = features.shape[0]
    modes, channels = residue.shape
    taps = short_taps.shape[1]
    tap_reach = taps - 1

    earlier = shifted(features[tok_count - tap_reach :], 1)
    weight = gather_weight(w_out.T)

    extended = jnp.concatenate([earlier, features], axis=0)
    mixed_in = short_taps[:, 0, :] * features
    for tap in range(1, taps):
        mixed_in = mixed_in + short_taps[:, tap, :] * extended[tap_reach - tap : tap_reach - tap + tok_count]
    query_part, keyed, valued = mixed_in[:, 0, :], mixed_in[:, 1, :], mixed_in[:, 2, :]
    product = lax.reduce_precision(keyed * valued, **HIGH)
    scales = jnp.sqrt(-jnp.expm1(-2.0 * decay_rate))
    coeffs = residue * scales
    slab_decay = jnp.exp(-decay_rate * tok_count)

    state_ends, state_enter = local_states(product, decay_rate, False)
    state_ends, cot_block = lax.optimization_barrier((state_ends, cotangent))
    cot_rows = gather_columns(cot_block)
    state_outer, cot_rows = entering(state_ends, slab_decay, False, cot_rows)
    cot_order, cot_ring = to_gather_order(cot_rows), to_ring_order(cot_rows)
    state_outer, cot_order, cot_ring = lax.optimization_barrier((state_outer, cot_order, cot_ring))
    convolved = forward_output(product, decay_rate, coeffs, state_enter, state_outer).astype(BF16)
    gated = (query_part * convolved).astype(BF16)
    weight_term = lax.dot_general(cot_ring, gated, (((0,), (0,)), ((), ())), preferred_element_type=F32)
    weight, weight_term = lax.optimization_barrier((weight, weight_term.astype(BF16)))
    grad_weight = weight_grad(weight_term)

    grad_gated = lax.reduce_precision(jnp.dot(cot_order, weight, preferred_element_type=F32), **HIGH)
    grad_conv = lax.reduce_precision(grad_gated * query_part, **HIGH)
    adj_ends, adj_enter = local_states(grad_conv, decay_rate, True)
    sums_here = mode_sums(product, grad_conv, decay_rate, state_enter, state_outer)
    adj_outer, (sums_here, gated) = entering(adj_ends, slab_decay, True, (sums_here, gated))
    alpha_rows, beta_part, slopes = sums_here
    partial_out = lax.dot_general(gated, weight, (((1,), (1,)), ((), ())), preferred_element_type=F32)
    partial_out = from_gather_order(partial_out.astype(BF16))
    adj_outer, partial_out = lax.optimization_barrier((adj_outer, partial_out))
    mixed = lax.psum_scatter(partial_out, "tp", scatter_dimension=1, tiled=True)
    grad_product, beta_rows = backward_output(
        grad_conv, decay_rate, coeffs, adj_enter, adj_outer, slopes, beta_part
    )
    grad_product = grad_product.astype(BF16)

    grad_query = (grad_gated * convolved).astype(BF16)
    grad_key = (grad_product * valued).astype(BF16)
    grad_value = (grad_product * keyed).astype(BF16)
    grad_mixed_in = jnp.stack([grad_query, grad_key, grad_value], axis=1)
    later = shifted(grad_mixed_in[:tap_reach], -1)
    grad_ext = jnp.concatenate([grad_mixed_in, later], axis=0)
    grad_feat = short_taps[:, 0, :] * grad_mixed_in
    tap_terms = []
    for tap in range(taps):
        if tap:
            grad_feat = grad_feat + short_taps[:, tap, :] * grad_ext[tap : tap + tok_count]
        tap_terms.append(
            jnp.einsum(
                "tjc,tjc->jc",
                grad_mixed_in,
                extended[tap_reach - tap : tap_reach - tap + tok_count],
                preferred_element_type=F32,
            )
        )
    tap_rows = jnp.stack(tap_terms, axis=1).reshape(3 * taps, channels)
    spare = jnp.zeros((SLABS - 2 * modes - 3 * taps, channels), F32)
    sums = total_over_slabs(jnp.concatenate([alpha_rows.reshape(modes, channels), beta_rows.reshape(modes, channels), tap_rows, spare], axis=0))
    alpha_sum, beta_sum = sums[:modes], sums[modes : 2 * modes]
    grad_taps = sums[2 * modes : 2 * modes + 3 * taps].reshape(3, taps, channels)
    grad_residue = scales * alpha_sum
    grad_log_rate = decay_rate * (
        alpha_sum * residue * jnp.exp(-2.0 * decay_rate) / scales - jnp.exp(-decay_rate) * coeffs * beta_sum
    )
    return (mixed, grad_feat.astype(BF16), grad_weight, grad_taps, grad_residue, grad_log_rate)


def solution(mesh):
    parts = Mesh(mesh.devices.reshape(NX, NY, NZ, mesh.devices.shape[1]), ("xh", "y", "z", "tp"))
    return jax.shard_map(
        local,
        mesh=parts,
        in_specs=(
            P(SEQ, None, "tp"),
            P(None, None, "tp"),
            P(None, "tp"),
            P(None, "tp"),
            P("tp", SEQ),
            P(SEQ, "tp"),
        ),
        out_specs=(
            P(SEQ, "tp"),
            P(SEQ, None, "tp"),
            P("tp", SEQ),
            P(None, None, "tp"),
            P(None, "tp"),
            P(None, "tp"),
        ),
        check_vma=False,
    )
```

```python
import jax
import jax.numpy as jnp
from jax import lax
from jax.experimental import pallas as pl
from jax.experimental.pallas import tpu as pltpu
from jax.sharding import Mesh, PartitionSpec as P

F32 = jnp.float32
BF16 = jnp.bfloat16
SEQ = ("xh", "y", "z")
NX, NY, NZ = 2, 4, 8
SLABS = NX * NY * NZ
SUB = 8
LANES = 128
GROUPS = 1
HIGH = dict(exponent_bits=8, mantissa_bits=7)


def spread(row):
    return jnp.broadcast_to(row, (SUB, LANES))


def sub_index():
    return lax.broadcasted_iota(jnp.int32, (SUB, LANES), 0)


def earlier_sum(ends, decay):
    index = sub_index()

    def moved(value, by):
        return jnp.where(index >= by, pltpu.roll(value, by, 0), 0.0)

    total = moved(ends, 1)
    factor = decay
    for by in (1, 2, 4):
        total = total + factor * moved(total, by)
        factor = factor * factor
    return total


def later_sum(ends, decay):
    index = sub_index()

    def moved(value, by):
        return jnp.where(index < SUB - by, pltpu.roll(value, SUB - by, 0), 0.0)

    total = moved(ends, 1)
    factor = decay
    for by in (1, 2, 4):
        total = total + factor * moved(total, by)
        factor = factor * factor
    return total


def lane_groups(run):
    def kernel(*refs):
        width = refs[0].shape[1]
        for group in range(width // LANES):
            column = pl.program_id(0) * (width // LANES) + group
            run(pl.ds(group * LANES, LANES), column, *refs)

    return kernel


def decays(rate_ref, lanes, modes):
    return [spread(jnp.exp(-rate_ref[m : m + 1, lanes])) for m in modes]


def local_states_kernel(backward, lanes, column, signal_ref, rate_ref, end_ref, enter_ref):
    modes = rate_ref.shape[0]
    steps = signal_ref.shape[0] // SUB
    decay = decays(rate_ref, lanes, range(modes))

    def step(i, states):
        at = steps - 1 - i if backward else i
        value = signal_ref[pl.ds(at, SUB, stride=steps), lanes]
        return tuple(decay[m] * states[m] + value for m in range(modes))

    zero = jnp.zeros((SUB, LANES), F32)
    states = lax.fori_loop(0, steps, step, (zero,) * modes, unroll=8)
    index = sub_index().astype(F32)
    distance = index if backward else (SUB - 1.0) - index
    for m in range(modes):
        rate = spread(rate_ref[m : m + 1, lanes]) * steps
        weighted = jnp.exp(-rate * distance) * states[m]
        end_ref[m, pl.ds(column, 1), :] = jnp.sum(weighted, axis=0, keepdims=True)
        join = later_sum if backward else earlier_sum
        enter_ref[m, :, lanes] = join(states[m], jnp.exp(-rate))


def start_states(lanes, column, rate_ref, enter_ref, outer_ref, steps, backward, m):
    index = sub_index().astype(F32)
    distance = (SUB - 1.0) - index if backward else index
    rate = spread(rate_ref[m : m + 1, lanes]) * steps
    outer = spread(outer_ref[m, pl.ds(column, 1), :])
    return enter_ref[m, :, lanes] + jnp.exp(-rate * distance) * outer


def output_steps(backward, lanes, signal_ref, decay, coeff, start, out_ref):
    steps = signal_ref.shape[0] // SUB
    modes = len(decay)

    def step(i, states):
        at = steps - 1 - i if backward else i
        value = signal_ref[pl.ds(at, SUB, stride=steps), lanes]
        states = tuple(decay[m] * states[m] + value for m in range(modes))
        terms = [coeff[m] * states[m] for m in range(modes)]
        while len(terms) > 1:
            terms = [terms[j] + terms[j + 1] for j in range(0, len(terms), 2)]
        out_ref[pl.ds(at, SUB, stride=steps), lanes] = terms[0]
        return states

    lax.fori_loop(0, steps, step, start, unroll=4)


def forward_kernel(lanes, column, signal_ref, rate_ref, coeff_ref, enter_ref, outer_ref, out_ref):
    modes = rate_ref.shape[0]
    steps = signal_ref.shape[0] // SUB
    decay = decays(rate_ref, lanes, range(modes))
    coeff = [spread(coeff_ref[m : m + 1, lanes]) for m in range(modes)]
    start = tuple(
        start_states(lanes, column, rate_ref, enter_ref, outer_ref, steps, False, m) for m in range(modes)
    )
    output_steps(False, lanes, signal_ref, decay, coeff, start, out_ref)


def backward_kernel(
    lanes,
    column,
    signal_ref,
    rate_ref,
    coeff_ref,
    enter_ref,
    outer_ref,
    slope_ref,
    partial_ref,
    out_ref,
    beta_ref,
):
    modes = rate_ref.shape[0]
    steps = signal_ref.shape[0] // SUB
    decay = decays(rate_ref, lanes, range(modes))
    coeff = [spread(coeff_ref[m : m + 1, lanes]) for m in range(modes)]
    start = tuple(
        start_states(lanes, column, rate_ref, enter_ref, outer_ref, steps, True, m) for m in range(modes)
    )
    for m in range(modes):
        crossing = jnp.sum(decay[m] * slope_ref[m, :, lanes] * start[m], axis=0, keepdims=True)
        beta_ref[m, pl.ds(column, 1), :] = partial_ref[m, pl.ds(column, 1), :] + crossing
    output_steps(True, lanes, signal_ref, decay, coeff, start, out_ref)


def sums_kernel(
    lanes, column, signal_ref, grad_ref, rate_ref, enter_ref, outer_ref, alpha_ref, partial_ref, slope_ref
):
    modes = rate_ref.shape[0]
    steps = signal_ref.shape[0] // SUB
    zero = jnp.zeros((SUB, LANES), F32)
    group = 8
    for first in range(0, modes, group):
        decay = decays(rate_ref, lanes, range(first, first + group))
        start = tuple(
            start_states(lanes, column, rate_ref, enter_ref, outer_ref, steps, False, first + m)
            for m in range(group)
        )

        def step(i, carry):
            states, slopes, alphas, betas = carry
            value = signal_ref[pl.ds(i, SUB, stride=steps), lanes]
            grad = grad_ref[pl.ds(i, SUB, stride=steps), lanes]
            slopes = tuple(decay[m] * slopes[m] + states[m] for m in range(group))
            states = tuple(decay[m] * states[m] + value for m in range(group))
            alphas = tuple(alphas[m] + grad * states[m] for m in range(group))
            betas = tuple(betas[m] + grad * slopes[m] for m in range(group))
            return states, slopes, alphas, betas

        zeros = (zero,) * group
        _, slopes, alphas, betas = lax.fori_loop(0, steps, step, (start, zeros, zeros, zeros), unroll=4)
        for m in range(group):
            row = first + m
            alpha_ref[row, pl.ds(column, 1), :] = jnp.sum(alphas[m], axis=0, keepdims=True)
            partial_ref[row, pl.ds(column, 1), :] = jnp.sum(betas[m], axis=0, keepdims=True)
            slope_ref[row, :, lanes] = slopes[m]


def modal_call(body, name, work, inputs, outputs):
    tokens, channels = inputs[0][1].shape
    modes = inputs[-1][1].shape[0]
    block = LANES * GROUPS
    blocks = {
        "tokens": pl.BlockSpec((tokens, block), lambda c: (0, c)),
        "modes": pl.BlockSpec((modes, block), lambda c: (0, c)),
        "subs": pl.BlockSpec((modes, SUB, block), lambda c: (0, 0, c)),
        "rows": pl.BlockSpec((modes, channels // LANES, LANES), lambda c: (0, 0, 0)),
    }
    shapes = {
        "tokens": (tokens, channels),
        "subs": (modes, SUB, channels),
        "rows": (modes, channels // LANES, LANES),
    }
    return pl.pallas_call(
        lane_groups(body),
        name=name,
        grid=(channels // block,),
        in_specs=[blocks[kind] for kind, _ in inputs],
        out_specs=[blocks[kind] for kind in outputs],
        out_shape=[jax.ShapeDtypeStruct(shapes[kind], F32) for kind in outputs],
        cost_estimate=pl.CostEstimate(
            flops=work * modes * tokens * channels, transcendentals=0, bytes_accessed=8 * tokens * channels
        ),
    )(*[array for _, array in inputs])


def local_states(signal, rates, backward):
    return modal_call(
        lambda *refs: local_states_kernel(backward, *refs),
        "adjoint_ends" if backward else "state_ends",
        2,
        [("tokens", signal), ("modes", rates)],
        ["rows", "subs"],
    )


def forward_output(signal, rates, coeffs, enter, outer):
    inputs = [("tokens", signal), ("modes", rates), ("modes", coeffs), ("subs", enter), ("rows", outer)]
    return modal_call(forward_kernel, "modal_forward", 4, inputs, ["tokens"])[0]


def backward_output(signal, rates, coeffs, enter, outer, slopes, partial):
    inputs = [("tokens", signal), ("modes", rates), ("modes", coeffs), ("subs", enter), ("rows", outer)]
    inputs += [("subs", slopes), ("rows", partial)]
    return modal_call(backward_kernel, "modal_backward", 4, inputs, ["tokens", "rows"])


def mode_sums(signal, grads, rates, enter, outer):
    inputs = [("tokens", signal), ("tokens", grads), ("modes", rates), ("subs", enter), ("rows", outer)]
    return modal_call(sums_kernel, "mode_sums", 8, inputs, ["rows", "rows", "subs"])


def slab_scan_kernel(backward, ends_ref, decay_ref, out_ref):
    decay = decay_ref[...]
    state = jnp.zeros(decay.shape, F32)
    order = range(SLABS - 1, -1, -1) if backward else range(SLABS)
    for slab in order:
        out_ref[slab] = state
        state = decay * state + ends_ref[slab]


def entering(ends, slab_decay, backward, beside):
    shape = (SLABS, ends.size // SLABS // LANES, LANES)
    mine = lax.axis_index(SEQ)
    decay = lax.dynamic_index_in_dim(slab_decay.reshape(shape), mine, 0, keepdims=False)
    gathered = lax.all_to_all(ends.reshape(shape), SEQ, 0, 0, tiled=True)
    gathered, beside = lax.optimization_barrier((gathered, beside))
    scanned = pl.pallas_call(
        lambda *refs: slab_scan_kernel(backward, *refs),
        name="slab_scan_back" if backward else "slab_scan",
        out_shape=jax.ShapeDtypeStruct(shape, F32),
        cost_estimate=pl.CostEstimate(
            flops=2 * ends.size, transcendentals=0, bytes_accessed=8 * ends.size
        ),
    )(gathered, decay)
    outer = lax.all_to_all(scanned, SEQ, 0, 0, tiled=True).reshape(ends.shape)
    return outer, beside


def ring(array, axis, size, by):
    return lax.ppermute(array, axis, [(i, (i + by) % size) for i in range(size)])


def gather_weight(w_rows):
    other = ring(w_rows, "xh", NX, 1)
    first = lax.axis_index("xh") == 0
    pair = jnp.concatenate([jnp.where(first, w_rows, other), jnp.where(first, other, w_rows)], axis=0)
    return lax.all_gather(pair, ("y", "z"), axis=0, tiled=True)


def to_gather_order(rows):
    tokens, width = rows.shape
    cols = width // SLABS
    return rows.reshape(tokens, NX, NY * NZ, cols).transpose(0, 2, 1, 3).reshape(tokens, width)


def from_gather_order(rows):
    tokens, width = rows.shape
    cols = width // SLABS
    return rows.reshape(tokens, NY * NZ, NX, cols).transpose(0, 2, 1, 3).reshape(tokens, width)


def gather_columns(block):
    size = lax.axis_size("tp")
    width = block.shape[1]
    own = lax.axis_index("tp")
    whole = jnp.zeros((block.shape[0], size * width), block.dtype)
    for offset in range(size):
        part = ring(block, "tp", size, -offset) if offset else block
        whole = lax.dynamic_update_slice_in_dim(whole, part, (own + offset) % size * width, 1)
    return whole


def shifted(array, by):
    pairs = [(i, i + by) for i in range(SLABS) if 0 <= i + by < SLABS]
    return lax.ppermute(array, SEQ, pairs)


def x_pair(cot_rows):
    tokens, width = cot_rows.shape
    side, cols = width // NX, width // SLABS
    mine = lax.axis_index("xh")

    def half(which):
        columns = lax.dynamic_slice_in_dim(cot_rows, which * side, side, 1)
        return columns.reshape(tokens, NY, NZ, cols).transpose(0, 2, 1, 3).reshape(tokens, side)

    return jnp.concatenate([half(mine), ring(half(1 - mine), "xh", NX, 1)], axis=0)


def weight_grad(term):
    summed = lax.psum_scatter(term, "z", scatter_dimension=0, tiled=True)
    by_y = summed.reshape(NY, -1, summed.shape[1])
    own = lax.axis_index("y")

    def block(target):
        return lax.dynamic_index_in_dim(by_y, target % NY, 0, keepdims=False)

    total = block(own).astype(F32)
    for offset in range(1, NY):
        total = total + ring(block(own - offset), "y", NY, -offset).astype(F32)
    return total


def total_over_slabs(rows):
    count, channels = rows.shape
    shape = (SLABS, count * channels // SLABS // LANES, LANES)
    pieces = lax.all_to_all(rows.reshape(shape), SEQ, 0, 0, tiled=True)
    summed = jnp.sum(pieces, axis=0)
    copies = jnp.broadcast_to(summed[None], shape)
    return lax.all_to_all(copies, SEQ, 0, 0, tiled=True).reshape(count, channels)


def local(features, short_taps, residue, decay_rate, w_out, cotangent):
    tok_count = features.shape[0]
    modes, channels = residue.shape
    taps = short_taps.shape[1]
    tap_reach = taps - 1

    earlier = shifted(features[tok_count - tap_reach :], 1)
    weight = gather_weight(w_out.T)

    extended = jnp.concatenate([earlier, features], axis=0)
    mixed_in = short_taps[:, 0, :] * features
    for tap in range(1, taps):
        mixed_in = mixed_in + short_taps[:, tap, :] * extended[tap_reach - tap : tap_reach - tap + tok_count]
    query_part, keyed, valued = mixed_in[:, 0, :], mixed_in[:, 1, :], mixed_in[:, 2, :]
    product = lax.reduce_precision(keyed * valued, **HIGH)
    scales = jnp.sqrt(-jnp.expm1(-2.0 * decay_rate))
    coeffs = residue * scales
    slab_decay = jnp.exp(-decay_rate * tok_count)

    state_ends, state_enter = local_states(product, decay_rate, False)
    state_ends, cot_block = lax.optimization_barrier((state_ends, cotangent))
    cot_rows = gather_columns(cot_block)
    state_outer, cot_rows = entering(state_ends, slab_decay, False, cot_rows)
    cot_order, cot_pair = to_gather_order(cot_rows), x_pair(cot_rows)
    state_outer, cot_order = lax.optimization_barrier((state_outer, cot_order))
    convolved = forward_output(product, decay_rate, coeffs, state_enter, state_outer).astype(BF16)
    convolved, cot_pair = lax.optimization_barrier((convolved, cot_pair))
    gated = (query_part * convolved).astype(BF16)
    grad_gated = lax.reduce_precision(jnp.dot(cot_order, weight, preferred_element_type=F32), **HIGH)
    grad_conv = lax.reduce_precision(grad_gated * query_part, **HIGH)
    grad_conv, gated = lax.optimization_barrier((grad_conv, gated))
    gated_pair = jnp.concatenate([gated, ring(gated, "xh", NX, 1)], axis=0)
    adj_ends, adj_enter = local_states(grad_conv, decay_rate, True)
    sums_here = mode_sums(product, grad_conv, decay_rate, state_enter, state_outer)
    adj_ends, cot_pair = lax.optimization_barrier((adj_ends, cot_pair))
    weight_term = lax.dot_general(cot_pair, gated_pair, (((0,), (0,)), ((), ())), preferred_element_type=F32)
    weight_term = weight_term.astype(BF16)
    weight_sum = weight_grad(weight_term)
    beside = (weight_term, sums_here, gated)
    adj_outer, (_, sums_here, gated) = entering(adj_ends, slab_decay, True, beside)
    alpha_rows, beta_part, slopes = sums_here
    partial_out = lax.dot_general(gated, weight, (((1,), (1,)), ((), ())), preferred_element_type=F32)
    partial_out = from_gather_order(partial_out.astype(BF16))
    adj_outer, partial_out = lax.optimization_barrier((adj_outer, partial_out))
    grad_product, beta_rows = backward_output(
        grad_conv, decay_rate, coeffs, adj_enter, adj_outer, slopes, beta_part
    )
    grad_product = grad_product.astype(BF16)
    mixed = lax.psum_scatter(partial_out, "tp", scatter_dimension=1, tiled=True)

    grad_query = (grad_gated * convolved).astype(BF16)
    grad_key = (grad_product * valued).astype(BF16)
    grad_value = (grad_product * keyed).astype(BF16)
    grad_mixed_in = jnp.stack([grad_query, grad_key, grad_value], axis=1)
    later = shifted(grad_mixed_in[:tap_reach], -1)
    grad_ext = jnp.concatenate([grad_mixed_in, later], axis=0)
    grad_feat = short_taps[:, 0, :] * grad_mixed_in
    tap_terms = []
    for tap in range(taps):
        if tap:
            grad_feat = grad_feat + short_taps[:, tap, :] * grad_ext[tap : tap + tok_count]
        tap_terms.append(
            jnp.einsum(
                "tjc,tjc->jc",
                grad_mixed_in,
                extended[tap_reach - tap : tap_reach - tap + tok_count],
                preferred_element_type=F32,
            )
        )
    tap_rows = jnp.stack(tap_terms, axis=1).reshape(3 * taps, channels)
    spare = jnp.zeros((SLABS - 2 * modes - 3 * taps, channels), F32)
    rows = jnp.concatenate([alpha_rows.reshape(modes, channels), beta_rows.reshape(modes, channels), tap_rows, spare])
    sums, weight_sum = lax.optimization_barrier((total_over_slabs(rows), weight_sum))
    grad_weight = weight_sum.T
    alpha_sum, beta_sum = sums[:modes], sums[modes : 2 * modes]
    grad_taps = sums[2 * modes : 2 * modes + 3 * taps].reshape(3, taps, channels)
    grad_residue = scales * alpha_sum
    grad_log_rate = decay_rate * (
        alpha_sum * residue * jnp.exp(-2.0 * decay_rate) / scales - jnp.exp(-decay_rate) * coeffs * beta_sum
    )
    return (mixed, grad_feat.astype(BF16), grad_weight, grad_taps, grad_residue, grad_log_rate)


def solution(mesh):
    parts = Mesh(mesh.devices.reshape(NX, NY, NZ, mesh.devices.shape[1]), ("xh", "y", "z", "tp"))
    return jax.shard_map(
        local,
        mesh=parts,
        in_specs=(
            P(SEQ, None, "tp"),
            P(None, None, "tp"),
            P(None, "tp"),
            P(None, "tp"),
            P("tp", SEQ),
            P(SEQ, "tp"),
        ),
        out_specs=(
            P(SEQ, "tp"),
            P(SEQ, None, "tp"),
            P("tp", SEQ),
            P(None, None, "tp"),
            P(None, "tp"),
            P(None, "tp"),
        ),
        check_vma=False,
    )
```

```python
import jax
import jax.numpy as jnp
from jax import lax
from jax.experimental import pallas as pl
from jax.experimental.pallas import tpu as pltpu
from jax.sharding import Mesh, PartitionSpec as P

F32 = jnp.float32
BF16 = jnp.bfloat16
SEQ = ("xh", "y", "z")
NX, NY, NZ = 2, 4, 8
SLABS = NX * NY * NZ
SUB = 8
LANES = 128
GROUPS = 1
HIGH = dict(exponent_bits=8, mantissa_bits=7)


def spread(row):
    return jnp.broadcast_to(row, (SUB, LANES))


def sub_index():
    return lax.broadcasted_iota(jnp.int32, (SUB, LANES), 0)


def earlier_sum(ends, decay):
    index = sub_index()

    def moved(value, by):
        return jnp.where(index >= by, pltpu.roll(value, by, 0), 0.0)

    total = moved(ends, 1)
    factor = decay
    for by in (1, 2, 4):
        total = total + factor * moved(total, by)
        factor = factor * factor
    return total


def later_sum(ends, decay):
    index = sub_index()

    def moved(value, by):
        return jnp.where(index < SUB - by, pltpu.roll(value, SUB - by, 0), 0.0)

    total = moved(ends, 1)
    factor = decay
    for by in (1, 2, 4):
        total = total + factor * moved(total, by)
        factor = factor * factor
    return total


def lane_groups(run):
    def kernel(*refs):
        width = refs[0].shape[1]
        for group in range(width // LANES):
            column = pl.program_id(0) * (width // LANES) + group
            run(pl.ds(group * LANES, LANES), column, *refs)

    return kernel


def decays(rate_ref, lanes, modes):
    return [spread(jnp.exp(-rate_ref[m : m + 1, lanes])) for m in modes]


def local_states_kernel(backward, lanes, column, signal_ref, rate_ref, end_ref, enter_ref):
    modes = rate_ref.shape[0]
    steps = signal_ref.shape[0] // SUB
    decay = decays(rate_ref, lanes, range(modes))

    def step(i, states):
        at = steps - 1 - i if backward else i
        value = signal_ref[pl.ds(at, SUB, stride=steps), lanes]
        return tuple(decay[m] * states[m] + value for m in range(modes))

    zero = jnp.zeros((SUB, LANES), F32)
    states = lax.fori_loop(0, steps, step, (zero,) * modes, unroll=8)
    index = sub_index().astype(F32)
    distance = index if backward else (SUB - 1.0) - index
    for m in range(modes):
        rate = spread(rate_ref[m : m + 1, lanes]) * steps
        weighted = jnp.exp(-rate * distance) * states[m]
        end_ref[m, pl.ds(column, 1), :] = jnp.sum(weighted, axis=0, keepdims=True)
        join = later_sum if backward else earlier_sum
        enter_ref[m, :, lanes] = join(states[m], jnp.exp(-rate))


def start_states(lanes, column, rate_ref, enter_ref, outer_ref, steps, backward, m):
    index = sub_index().astype(F32)
    distance = (SUB - 1.0) - index if backward else index
    rate = spread(rate_ref[m : m + 1, lanes]) * steps
    outer = spread(outer_ref[m, pl.ds(column, 1), :])
    return enter_ref[m, :, lanes] + jnp.exp(-rate * distance) * outer


def output_steps(backward, lanes, signal_ref, decay, coeff, start, out_ref):
    steps = signal_ref.shape[0] // SUB
    modes = len(decay)

    def step(i, states):
        at = steps - 1 - i if backward else i
        value = signal_ref[pl.ds(at, SUB, stride=steps), lanes]
        states = tuple(decay[m] * states[m] + value for m in range(modes))
        terms = [coeff[m] * states[m] for m in range(modes)]
        while len(terms) > 1:
            terms = [terms[j] + terms[j + 1] for j in range(0, len(terms), 2)]
        out_ref[pl.ds(at, SUB, stride=steps), lanes] = terms[0]
        return states

    lax.fori_loop(0, steps, step, start, unroll=4)


def forward_kernel(lanes, column, signal_ref, rate_ref, coeff_ref, enter_ref, outer_ref, out_ref):
    modes = rate_ref.shape[0]
    steps = signal_ref.shape[0] // SUB
    decay = decays(rate_ref, lanes, range(modes))
    coeff = [spread(coeff_ref[m : m + 1, lanes]) for m in range(modes)]
    start = tuple(
        start_states(lanes, column, rate_ref, enter_ref, outer_ref, steps, False, m) for m in range(modes)
    )
    output_steps(False, lanes, signal_ref, decay, coeff, start, out_ref)


def backward_kernel(
    lanes,
    column,
    signal_ref,
    rate_ref,
    coeff_ref,
    enter_ref,
    outer_ref,
    slope_ref,
    partial_ref,
    out_ref,
    beta_ref,
):
    modes = rate_ref.shape[0]
    steps = signal_ref.shape[0] // SUB
    decay = decays(rate_ref, lanes, range(modes))
    coeff = [spread(coeff_ref[m : m + 1, lanes]) for m in range(modes)]
    start = tuple(
        start_states(lanes, column, rate_ref, enter_ref, outer_ref, steps, True, m) for m in range(modes)
    )
    for m in range(modes):
        crossing = jnp.sum(decay[m] * slope_ref[m, :, lanes] * start[m], axis=0, keepdims=True)
        beta_ref[m, pl.ds(column, 1), :] = partial_ref[m, pl.ds(column, 1), :] + crossing
    output_steps(True, lanes, signal_ref, decay, coeff, start, out_ref)


def sums_kernel(
    lanes, column, signal_ref, grad_ref, rate_ref, enter_ref, outer_ref, alpha_ref, partial_ref, slope_ref
):
    modes = rate_ref.shape[0]
    steps = signal_ref.shape[0] // SUB
    zero = jnp.zeros((SUB, LANES), F32)
    group = 8
    for first in range(0, modes, group):
        decay = decays(rate_ref, lanes, range(first, first + group))
        start = tuple(
            start_states(lanes, column, rate_ref, enter_ref, outer_ref, steps, False, first + m)
            for m in range(group)
        )

        def step(i, carry):
            states, slopes, alphas, betas = carry
            value = signal_ref[pl.ds(i, SUB, stride=steps), lanes]
            grad = grad_ref[pl.ds(i, SUB, stride=steps), lanes]
            slopes = tuple(decay[m] * slopes[m] + states[m] for m in range(group))
            states = tuple(decay[m] * states[m] + value for m in range(group))
            alphas = tuple(alphas[m] + grad * states[m] for m in range(group))
            betas = tuple(betas[m] + grad * slopes[m] for m in range(group))
            return states, slopes, alphas, betas

        zeros = (zero,) * group
        _, slopes, alphas, betas = lax.fori_loop(0, steps, step, (start, zeros, zeros, zeros), unroll=4)
        for m in range(group):
            row = first + m
            alpha_ref[row, pl.ds(column, 1), :] = jnp.sum(alphas[m], axis=0, keepdims=True)
            partial_ref[row, pl.ds(column, 1), :] = jnp.sum(betas[m], axis=0, keepdims=True)
            slope_ref[row, :, lanes] = slopes[m]


def modal_call(body, name, work, inputs, outputs):
    tokens, channels = inputs[0][1].shape
    modes = inputs[-1][1].shape[0]
    block = LANES * GROUPS
    blocks = {
        "tokens": pl.BlockSpec((tokens, block), lambda c: (0, c)),
        "modes": pl.BlockSpec((modes, block), lambda c: (0, c)),
        "subs": pl.BlockSpec((modes, SUB, block), lambda c: (0, 0, c)),
        "rows": pl.BlockSpec((modes, channels // LANES, LANES), lambda c: (0, 0, 0)),
    }
    shapes = {
        "tokens": (tokens, channels),
        "subs": (modes, SUB, channels),
        "rows": (modes, channels // LANES, LANES),
    }
    return pl.pallas_call(
        lane_groups(body),
        name=name,
        grid=(channels // block,),
        in_specs=[blocks[kind] for kind, _ in inputs],
        out_specs=[blocks[kind] for kind in outputs],
        out_shape=[jax.ShapeDtypeStruct(shapes[kind], F32) for kind in outputs],
        cost_estimate=pl.CostEstimate(
            flops=work * modes * tokens * channels, transcendentals=0, bytes_accessed=8 * tokens * channels
        ),
    )(*[array for _, array in inputs])


def local_states(signal, rates, backward):
    return modal_call(
        lambda *refs: local_states_kernel(backward, *refs),
        "adjoint_ends" if backward else "state_ends",
        2,
        [("tokens", signal), ("modes", rates)],
        ["rows", "subs"],
    )


def forward_output(signal, rates, coeffs, enter, outer):
    inputs = [("tokens", signal), ("modes", rates), ("modes", coeffs), ("subs", enter), ("rows", outer)]
    return modal_call(forward_kernel, "modal_forward", 4, inputs, ["tokens"])[0]


def backward_output(signal, rates, coeffs, enter, outer, slopes, partial):
    inputs = [("tokens", signal), ("modes", rates), ("modes", coeffs), ("subs", enter), ("rows", outer)]
    inputs += [("subs", slopes), ("rows", partial)]
    return modal_call(backward_kernel, "modal_backward", 4, inputs, ["tokens", "rows"])


def mode_sums(signal, grads, rates, enter, outer):
    inputs = [("tokens", signal), ("tokens", grads), ("modes", rates), ("subs", enter), ("rows", outer)]
    return modal_call(sums_kernel, "mode_sums", 8, inputs, ["rows", "rows", "subs"])


def slab_scan_kernel(backward, ends_ref, decay_ref, out_ref):
    decay = decay_ref[...]
    state = jnp.zeros(decay.shape, F32)
    order = range(SLABS - 1, -1, -1) if backward else range(SLABS)
    for slab in order:
        out_ref[slab] = state
        state = decay * state + ends_ref[slab]


def entering(ends, slab_decay, backward, beside):
    shape = (SLABS, ends.size // SLABS // LANES, LANES)
    mine = lax.axis_index(SEQ)
    decay = lax.dynamic_index_in_dim(slab_decay.reshape(shape), mine, 0, keepdims=False)
    gathered = lax.all_to_all(ends.reshape(shape), SEQ, 0, 0, tiled=True)
    gathered, beside = lax.optimization_barrier((gathered, beside))
    scanned = pl.pallas_call(
        lambda *refs: slab_scan_kernel(backward, *refs),
        name="slab_scan_back" if backward else "slab_scan",
        out_shape=jax.ShapeDtypeStruct(shape, F32),
        cost_estimate=pl.CostEstimate(
            flops=2 * ends.size, transcendentals=0, bytes_accessed=8 * ends.size
        ),
    )(gathered, decay)
    outer = lax.all_to_all(scanned, SEQ, 0, 0, tiled=True).reshape(ends.shape)
    return outer, beside


def ring(array, axis, size, by):
    return lax.ppermute(array, axis, [(i, (i + by) % size) for i in range(size)])


def gather_weight(w_rows):
    other = ring(w_rows, "xh", NX, 1)
    first = lax.axis_index("xh") == 0
    pair = jnp.concatenate([jnp.where(first, w_rows, other), jnp.where(first, other, w_rows)], axis=0)
    return lax.all_gather(pair, ("y", "z"), axis=0, tiled=True)


def to_gather_order(rows):
    tokens, width = rows.shape
    cols = width // SLABS
    return rows.reshape(tokens, NX, NY * NZ, cols).transpose(0, 2, 1, 3).reshape(tokens, width)


def from_gather_order(rows):
    tokens, width = rows.shape
    cols = width // SLABS
    return rows.reshape(tokens, NY * NZ, NX, cols).transpose(0, 2, 1, 3).reshape(tokens, width)


def gather_columns(block):
    size = lax.axis_size("tp")
    width = block.shape[1]
    own = lax.axis_index("tp")
    whole = jnp.zeros((block.shape[0], size * width), block.dtype)
    for offset in range(size):
        part = ring(block, "tp", size, -offset) if offset else block
        whole = lax.dynamic_update_slice_in_dim(whole, part, (own + offset) % size * width, 1)
    return whole


def shifted(array, by):
    pairs = [(i, i + by) for i in range(SLABS) if 0 <= i + by < SLABS]
    return lax.ppermute(array, SEQ, pairs)


def x_pair(cot_rows):
    tokens, width = cot_rows.shape
    side, cols = width // NX, width // SLABS
    mine = lax.axis_index("xh")

    def half(which):
        columns = lax.dynamic_slice_in_dim(cot_rows, which * side, side, 1)
        return columns.reshape(tokens, NY, NZ, cols).transpose(0, 2, 1, 3).reshape(tokens, side)

    return jnp.concatenate([half(mine), ring(half(1 - mine), "xh", NX, 1)], axis=0)


def weight_grad(term):
    summed = lax.psum_scatter(term, "z", scatter_dimension=0, tiled=True)
    by_y = summed.reshape(NY, -1, summed.shape[1])
    own = lax.axis_index("y")

    def block(target):
        return lax.dynamic_index_in_dim(by_y, target % NY, 0, keepdims=False)

    total = block(own).astype(F32)
    for offset in range(1, NY):
        total = total + ring(block(own - offset), "y", NY, -offset).astype(F32)
    return total


def total_over_slabs(rows):
    count, channels = rows.shape
    shape = (SLABS, count * channels // SLABS // LANES, LANES)
    pieces = lax.all_to_all(rows.reshape(shape), SEQ, 0, 0, tiled=True)
    summed = jnp.sum(pieces, axis=0)
    copies = jnp.broadcast_to(summed[None], shape)
    return lax.all_to_all(copies, SEQ, 0, 0, tiled=True).reshape(count, channels)


def local(features, short_taps, residue, decay_rate, w_out, cotangent):
    tok_count = features.shape[0]
    modes, channels = residue.shape
    taps = short_taps.shape[1]
    tap_reach = taps - 1

    earlier = shifted(features[tok_count - tap_reach :], 1)
    weight = gather_weight(w_out.T)

    extended = jnp.concatenate([earlier, features], axis=0)
    mixed_in = short_taps[:, 0, :] * features
    for tap in range(1, taps):
        mixed_in = mixed_in + short_taps[:, tap, :] * extended[tap_reach - tap : tap_reach - tap + tok_count]
    query_part, keyed, valued = mixed_in[:, 0, :], mixed_in[:, 1, :], mixed_in[:, 2, :]
    product = lax.reduce_precision(keyed * valued, **HIGH)
    scales = jnp.sqrt(-jnp.expm1(-2.0 * decay_rate))
    coeffs = residue * scales
    slab_decay = jnp.exp(-decay_rate * tok_count)

    state_ends, state_enter = local_states(product, decay_rate, False)
    state_ends, cot_block = lax.optimization_barrier((state_ends, cotangent))
    cot_rows = gather_columns(cot_block)
    state_outer, cot_rows = entering(state_ends, slab_decay, False, cot_rows)
    cot_order, cot_pair = to_gather_order(cot_rows), x_pair(cot_rows)
    state_outer, cot_order = lax.optimization_barrier((state_outer, cot_order))
    convolved = forward_output(product, decay_rate, coeffs, state_enter, state_outer).astype(BF16)
    convolved, cot_pair = lax.optimization_barrier((convolved, cot_pair))
    gated = (query_part * convolved).astype(BF16)
    grad_gated = lax.reduce_precision(jnp.dot(cot_order, weight, preferred_element_type=F32), **HIGH)
    grad_conv = lax.reduce_precision(grad_gated * query_part, **HIGH)
    grad_conv, gated = lax.optimization_barrier((grad_conv, gated))
    gated_pair = jnp.concatenate([gated, ring(gated, "xh", NX, 1)], axis=0)
    adj_ends, adj_enter = local_states(grad_conv, decay_rate, True)
    sums_here = mode_sums(product, grad_conv, decay_rate, state_enter, state_outer)
    adj_ends, cot_pair = lax.optimization_barrier((adj_ends, cot_pair))
    weight_term = lax.dot_general(cot_pair, gated_pair, (((0,), (0,)), ((), ())), preferred_element_type=F32)
    weight_term = weight_term.astype(BF16)
    weight_sum = weight_grad(weight_term)
    beside = (weight_term, sums_here, gated)
    adj_outer, (_, sums_here, gated) = entering(adj_ends, slab_decay, True, beside)
    alpha_rows, beta_part, slopes = sums_here
    partial_out = lax.dot_general(gated, weight, (((1,), (1,)), ((), ())), preferred_element_type=F32)
    adj_outer, partial_out = lax.optimization_barrier((adj_outer, partial_out.astype(BF16)))
    grad_product, beta_rows = backward_output(
        grad_conv, decay_rate, coeffs, adj_enter, adj_outer, slopes, beta_part
    )
    grad_product = grad_product.astype(BF16)
    mixed = lax.psum_scatter(from_gather_order(partial_out), "tp", scatter_dimension=1, tiled=True)

    grad_query = (grad_gated * convolved).astype(BF16)
    grad_key = (grad_product * valued).astype(BF16)
    grad_value = (grad_product * keyed).astype(BF16)
    grad_mixed_in = jnp.stack([grad_query, grad_key, grad_value], axis=1)
    later = shifted(grad_mixed_in[:tap_reach], -1)
    grad_ext = jnp.concatenate([grad_mixed_in, later], axis=0)
    grad_feat = short_taps[:, 0, :] * grad_mixed_in
    tap_terms = []
    for tap in range(taps):
        if tap:
            grad_feat = grad_feat + short_taps[:, tap, :] * grad_ext[tap : tap + tok_count]
        tap_terms.append(
            jnp.einsum(
                "tjc,tjc->jc",
                grad_mixed_in,
                extended[tap_reach - tap : tap_reach - tap + tok_count],
                preferred_element_type=F32,
            )
        )
    tap_rows = jnp.stack(tap_terms, axis=1).reshape(3 * taps, channels)
    spare = jnp.zeros((SLABS - 2 * modes - 3 * taps, channels), F32)
    rows = jnp.concatenate([alpha_rows.reshape(modes, channels), beta_rows.reshape(modes, channels), tap_rows, spare])
    sums, weight_sum = lax.optimization_barrier((total_over_slabs(rows), weight_sum))
    grad_weight = weight_sum.T
    alpha_sum, beta_sum = sums[:modes], sums[modes : 2 * modes]
    grad_taps = sums[2 * modes : 2 * modes + 3 * taps].reshape(3, taps, channels)
    grad_residue = scales * alpha_sum
    grad_log_rate = decay_rate * (
        alpha_sum * residue * jnp.exp(-2.0 * decay_rate) / scales - jnp.exp(-decay_rate) * coeffs * beta_sum
    )
    return (mixed, grad_feat.astype(BF16), grad_weight, grad_taps, grad_residue, grad_log_rate)


def solution(mesh):
    parts = Mesh(mesh.devices.reshape(NX, NY, NZ, mesh.devices.shape[1]), ("xh", "y", "z", "tp"))
    return jax.shard_map(
        local,
        mesh=parts,
        in_specs=(
            P(SEQ, None, "tp"),
            P(None, None, "tp"),
            P(None, "tp"),
            P(None, "tp"),
            P("tp", SEQ),
            P(SEQ, "tp"),
        ),
        out_specs=(
            P(SEQ, "tp"),
            P(SEQ, None, "tp"),
            P("tp", SEQ),
            P(None, None, "tp"),
            P(None, "tp"),
            P(None, "tp"),
        ),
        check_vma=False,
    )
```
